512 devices in a mesh: dp: 128 (over y, z, core), rep: 4 (over x).
Axes of the slice: x: 4, y: 8, z: 8, core: 2. Of those that a mesh axis runs over, the one named last changes fastest.
Arguments:
- hot_ids: int32 [65536, 13], P(('dp', 'rep')), may hold values from 0 to 1023
- cold_rows: int32 [65536, 13], P(('dp', 'rep')), may hold values from 0 to 2047
- cold_owner: int32 [851968, 1], P(('dp', 'rep')), may hold values from 0 to 127; in each aligned block of 1664 rows (0 to 1663, 1664 to 3327, ...) at most 26 rows name the same one
- labels: int32 [65536], P(('dp', 'rep')), may hold values 0 or 1
- hot_table: float32 [1024, 128], replicated, may hold values from -6 to 6
- hot_backup: bfloat16 [1024, 128], replicated, may hold values from -6 to 6
- cold_table: float32 [262144, 128], P('dp'), may hold values from -6 to 6
- cold_backup: bfloat16 [262144, 128], P('dp'), may hold values from -6 to 6
- cross_down: bfloat16 [3328, 512], P(None, ('dp', 'rep')), may hold values from -0.109375 to 0.109375
- cross_up: bfloat16 [512, 3328], P(('dp', 'rep')), may hold values from -0.25 to 0.25
- cross_bias: float32 [3328], replicated, may hold values from -3 to 3
- out_weight: float32 [3328], replicated, may hold values from -0.109375 to 0.109375
Outputs:
- new_hot: float32 [1024, 128], replicated
- new_cold: float32 [262144, 128], P('dp')
The draws below stay inside these ranges and needn't reach their ends.
Inputs may be any that keep to these rules, and one draw needn't show every extreme that they name: `cold_owner`: among the 1664 lookups of one device no owner is named more than 26 times, and in some device one owner is named exactly 26 times.
All inputs are finite; a program needn't handle non-finite values. No bound on the sum of `labels` on one device may be relied on, other than what follows from the above.
Results may differ from the reference program's by a relative error of at most 0.0028.
Values may be sent and summed in bfloat16 or wider, within the bound.
A program may use at most 64 MiB of HBM per device.

```python
import math
import jax
import jax.numpy as jnp
import numpy as np
from jax import lax

E = 128
NH = 13
NC = 13
R = 512
B_DEV = 128
HOT = 1024
COLD_DEV = 2048
F = 3328
BATCH = 65536
COLD_ROWS = 262144
CAP = 26
N_DP = 128
N_REP = 4


def set_ends(values, stream_key, low, largest):
    spot = [jax.random.randint(jax.random.fold_in(stream_key, axis), (), 0, length) for axis, length in enumerate(values.shape)]
    longest = values.shape.index(max(values.shape))
    beside = spot[:longest] + [(spot[longest] + 1) % values.shape[longest]] + spot[longest + 1:]
    return values.at[tuple(spot)].set(low).at[tuple(beside)].set(largest)


def steps_of(own_key, shape, cuts, smallest, high):
    level, own = 1.0, jax.random.fold_in(own_key, 6)
    for position, parts in cuts:
        heights = jnp.exp(jax.random.uniform(jax.random.fold_in(own, position), (parts,), jnp.float32, smallest / len(cuts), high / len(cuts)))
        level = level * jnp.repeat(heights, shape[position] // parts).reshape([-1 if axis == position else 1 for axis in range(len(shape))])
    return level


def rank_table(amount, skew):
    loads = [(1 << 20) // math.isqrt(grade ** skew) + 1 for grade in range(1, amount + 1)]
    scale = 1 + sum(loads) // (1 << 30)
    return np.cumsum(np.array([max(1, weight // scale) for weight in loads]))


def ranked_ids(stream_key, dims, count, skew):
    table = rank_table(count, skew)
    ticket = jax.random.randint(jax.random.fold_in(stream_key, 1), dims, 0, int(table[count - 1]))
    grade = jnp.searchsorted(jnp.asarray(table, jnp.int32), ticket, side="right")
    return jax.random.permutation(jax.random.fold_in(stream_key, 2), count)[grade].astype(jnp.int32)


def deal_out(stream_key, own, number, rows, number_of, top, bound, slope):
    sequence = jax.random.permutation(stream_key, number_of)
    crowded, common = load_shares(number_of, rows * top, bound, slope, True), load_shares(number_of, rows * top, bound, slope, False)
    places = jnp.arange(number_of)

    def named(tallies, rotation):
        used = int((tallies > 0).sum())
        fixed = max(1, used // 4)
        passed = fixed + (places - fixed + rotation * (used - fixed)) % max(1, number_of - fixed)
        return jnp.zeros((number_of,), jnp.int32).at[sequence[jnp.where(places < fixed, places, passed)]].set(jnp.asarray(tallies, jnp.int32))

    tallies = jnp.where(number % 4 == 0, named(crowded, number // 4), named(common, number - number // 4 - 1))
    mixed = jax.random.permutation(jax.random.fold_in(own, 3), number_of)
    source_of, taker = mixed[0:number_of // 2 * 2:2], mixed[1:number_of // 2 * 2:2]
    room = jnp.minimum(tallies[source_of] - 1, bound - tallies[taker]) // 2
    room = jnp.where((source_of == sequence[0]) | (taker == sequence[0]) | (tallies[taker] == 0), 0, jnp.maximum(room, 0))
    passed = jax.random.randint(jax.random.fold_in(own, 4), (number_of // 2,), 0, 1 << 20) % (room + 1)
    tallies = tallies.at[source_of].add(-passed).at[taker].add(passed)
    members = jnp.searchsorted(jnp.cumsum(tallies), jnp.arange(rows * top), side="right").astype(jnp.int32)
    grid = members.reshape(top, rows).T
    grid = grid[jax.random.permutation(jax.random.fold_in(own, 1), rows)]
    rotation = jax.random.randint(jax.random.fold_in(own, 2), (rows, 1), 0, top)
    return jnp.take_along_axis(grid, (jnp.arange(top)[None, :] + rotation) % top, axis=1)


def load_shares(number_of, total, most, slope, full):
    loads = [(1 << 20) // math.isqrt(rank ** slope) + 1 for rank in range(1, number_of + 1)]
    largest = most if full else min(most, max(-(-total // number_of), total * loads[0] // sum(loads)))
    least = 1 if total - largest >= number_of - 1 else 0
    given, rest = [largest] + [least] * (number_of - 1), total - largest - least * (number_of - 1)
    while rest > 0:
        candidates = [i for i in range(1, number_of) if given[i] < largest] or [i for i in range(1, number_of) if given[i] < most]
        pool, budget = sum([loads[i] for i in candidates]), rest
        for i in candidates:
            extra = min(most - given[i], max(1, budget * loads[i] // pool), rest)
            given[i] = given[i] + extra
            rest = rest - extra
    return np.array(given)


def noise(rng, extent, scale, most, shards=(), held_as=jnp.bfloat16):
    result = jax.random.normal(rng, extent, jnp.float32) * scale
    if len(shards) > 0:
        result = steps_of(rng, extent, shards, -0.22, 0.18) * result
    return jnp.clip(result, min=-most, max=most).astype(held_as)


def setup_inputs(seed: int = 0) -> dict:
    arg_keys = jax.random.split(jax.random.key(seed), 13)
    hot_ids = set_ends(ranked_ids(arg_keys[0], (BATCH, NH), HOT, 1), jax.random.fold_in(arg_keys[0], 3), 0, HOT - 1).astype(jnp.int32)
    cold_rows = set_ends(jax.random.randint(arg_keys[1], (BATCH, NC), 0, COLD_DEV), jax.random.fold_in(arg_keys[1], 1), 0, COLD_DEV - 1).astype(jnp.int32)
    cold_owner_keys = jax.random.split(jax.random.fold_in(arg_keys[2], 1), (BATCH * NC) // (B_DEV * NC))
    cold_owner_turns = jax.random.permutation(jax.random.fold_in(arg_keys[2], 3), (BATCH * NC) // (B_DEV * NC))
    cold_owner = jax.vmap(lambda own, number: deal_out(jax.random.fold_in(arg_keys[2], 2), own, number, B_DEV * NC, N_DP, 1, CAP, 2))(cold_owner_keys, cold_owner_turns).reshape((BATCH * NC, 1))
    labels = set_ends((jax.random.randint(arg_keys[3], (BATCH,), 0, 4) < 1).astype(jnp.int32), jax.random.fold_in(arg_keys[3], 1), 0, 1)
    hot_table = noise(arg_keys[4], (HOT, E), 1.0, 6.0, (), jnp.float32)
    hot_backup = noise(arg_keys[5], (HOT, E), 1.0, 6.0)
    cold_table = noise(arg_keys[6], (COLD_ROWS, E), 1.0, 6.0, ((0, 128),), jnp.float32)
    cold_backup = noise(arg_keys[7], (COLD_ROWS, E), 1.0, 6.0, ((0, 128),))
    cross_down = noise(arg_keys[8], (F, R), F ** -0.5, 0.109375, ((1, 512),))
    cross_up = noise(arg_keys[9], (R, F), R ** -0.5, 0.25, ((0, 512),))
    cross_bias = noise(arg_keys[10], (F,), 0.5, 3.0, (), jnp.float32)
    out_weight = noise(arg_keys[11], (F,), F ** -0.5, 0.109375, (), jnp.float32)
    return {"hot_ids": hot_ids, "cold_rows": cold_rows, "cold_owner": cold_owner, "labels": labels, "hot_table": hot_table, "hot_backup": hot_backup, "cold_table": cold_table, "cold_backup": cold_backup, "cross_down": cross_down, "cross_up": cross_up, "cross_bias": cross_bias, "out_weight": out_weight}


def block_grads(carry, inputs):
    hot_acc, cold_acc = carry
    hids, crow, cown, labs, hot_table, cold_table, cross_down, cross_up, cross_bias, out_weight = inputs
    rows = hids.shape[0]
    cold_id = (cown * COLD_DEV + crow).astype(jnp.int32)
    hot_emb = hot_table[hids].astype(jnp.bfloat16)
    cold_emb = cold_table[cold_id].astype(jnp.bfloat16)
    first = jnp.concatenate([hot_emb, cold_emb], axis=1).reshape(rows, F)
    hidden = jnp.dot(first, cross_down, preferred_element_type=jnp.float32).astype(jnp.bfloat16)
    upper = jnp.dot(hidden, cross_up, preferred_element_type=jnp.float32) + cross_bias[None, :]
    first_f = first.astype(jnp.float32)
    second = first_f * upper + first_f
    logit = lax.optimization_barrier(jnp.sum(second * out_weight[None, :], axis=1))
    delta = jax.nn.sigmoid(logit) - labs.astype(jnp.float32)
    d_second = delta[:, None] * out_weight[None, :]
    d_upper = (d_second * first_f).astype(jnp.bfloat16)
    d_hidden = jnp.dot(d_upper, cross_up.T, preferred_element_type=jnp.float32).astype(jnp.bfloat16)
    d_first = d_second * (upper + 1.0) + jnp.dot(d_hidden, cross_down.T, preferred_element_type=jnp.float32)
    grads = d_first.reshape(rows, NH + NC, E)
    hot_acc = hot_acc + jax.ops.segment_sum(grads[:, :NH].reshape(rows * NH, E), hids.reshape(-1), HOT)
    cold_low = lax.optimization_barrier(grads[:, NH:].astype(jnp.bfloat16))
    cold_acc = cold_acc + jax.ops.segment_sum(cold_low.astype(jnp.float32).reshape(rows * NC, E), cold_id.reshape(-1), COLD_ROWS)
    return (hot_acc, cold_acc)

def compensate(table, backup, grad, rate):
    step_size = rate * grad
    return table - step_size - 0.5 * step_size * step_size * (table - backup.astype(jnp.float32))

def reference(hot_ids, cold_rows, cold_owner, labels, hot_table, hot_backup, cold_table, cold_backup, cross_down, cross_up, cross_bias, out_weight):
    block = B_DEV * N_REP
    count = BATCH // block
    hids = hot_ids.reshape(count, block, NH)
    crow = cold_rows.reshape(count, block, NC)
    cown = cold_owner.reshape(count, block, NC)
    labs = labels.reshape(count, block)

    def step(carry, xs):
        return (block_grads(carry, (xs[0], xs[1], xs[2], xs[3], hot_table, cold_table, cross_down, cross_up, cross_bias, out_weight)), None)
    init = (jnp.zeros((HOT, E), jnp.float32), jnp.zeros((COLD_ROWS, E), jnp.float32))
    (hot_grad, cold_grad), unused = lax.scan(step, init, (hids, crow, cown, labs))
    rate_hot = 20.0 * math.sqrt(HOT / (BATCH * NH))
    rate_cold = 20.0 * math.sqrt(COLD_ROWS / (BATCH * NC))
    return (compensate(hot_table, hot_backup, hot_grad, rate_hot), compensate(cold_table, cold_backup, cold_grad, rate_cold))
```

```python
import math

import jax
import jax.numpy as jnp
from jax import lax
from jax.experimental import pallas as pl
from jax.experimental.pallas import tpu as pltpu
from jax.sharding import PartitionSpec as P

E = 128
NH = 13
NC = 13
HOT = 1024
F = 3328
R = 512
B = 128
OWN = 2048
SLOTS = 32
N_DP = 128
N_X = 4
N_Y = 8
N_Z = 8
LINE = 2 * N_Z
MESH = pl.DeviceIdType.MESH
F32 = jnp.float32
BF16 = jnp.bfloat16
I32 = jnp.int32

NT = (((1,), (1,)), ((), ()))


def remote(src, dst, send, recv, device):
    return pltpu.make_async_remote_copy(
        src_ref=src, dst_ref=dst, send_sem=send, recv_sem=recv, device_id=device, device_id_type=MESH
    )


def iota(shape, dim):
    return lax.broadcasted_iota(I32, shape, dim)


def enter(me, x, others):
    barrier = pltpu.get_barrier_semaphore()

    def greet(k, carry):
        pl.semaphore_signal(barrier, inc=1, device_id=(lax.rem(me + k, N_DP), x), device_id_type=MESH)
        return carry

    lax.fori_loop(1, N_DP, greet, 0)
    for step in others:
        pl.semaphore_signal(barrier, inc=1, device_id=(me, lax.rem(x + step, N_X)), device_id_type=MESH)
    pl.semaphore_wait(barrier, N_DP - 1 + len(others))


def fetch_kernel(
    owner_ref, rows_ref, shard_ref, table_ref,
    ret, weights, asked, place_ref,
    req, low_table, snd, line,
    req_s, req_r, row_s, row_r, line_s, line_r,
    up_s, up_r, dn_s, dn_r, xp_s, xp_r, xm_s, xm_r, x2_s, x2_r, sib_s, sib_r,
):
    me = lax.axis_index("dp")
    x = lax.axis_index("rep")
    y = me // LINE
    spot = lax.rem(me, LINE)
    core = lax.rem(me, 2)
    sibling = (me + 1 - 2 * core, x)
    enter(me, x, (1, N_X - 1))

    def line_send(k, carry):
        to = lax.rem(spot + k, LINE)
        remote(shard_ref.at[lax.rem(to, 2)], line.at[spot], line_s, line_r, (y * LINE + to, x)).start()
        return carry

    lax.fori_loop(1, LINE, line_send, 0)
    line[pl.ds(spot, 1)] = shard_ref[pl.ds(core, 1)]

    sub = iota((B, B), 0)
    lane = iota((B, B), 1)
    before = jnp.where(sub < lane, 1.0, 0.0).astype(BF16)
    count = jnp.zeros((N_DP, 1), F32)
    high = jnp.zeros((N_DP, B), F32)
    low = jnp.zeros((N_DP, B), F32)
    corner = SLOTS * lax.rem(me, 4)
    for j in range(NC):
        own = owner_ref[j : j + 1, :]
        value = rows_ref[j : j + 1, :] + 1
        hit = sub == own
        hit_f = jnp.where(hit, 1.0, 0.0)
        rank = jnp.dot(hit_f.astype(BF16), before, preferred_element_type=F32) + count
        slot = jnp.sum(hit_f * rank, axis=0, keepdims=True).astype(I32)
        count = count + jnp.sum(hit_f, axis=1, keepdims=True)
        place_ref[j : j + 1, :] = own * SLOTS + slot
        at = jnp.where(sub == slot + corner, 1.0, 0.0).astype(BF16)
        top = (hit_f * (value >> 5).astype(F32)).astype(BF16)
        rest = (hit_f * (value & 31).astype(F32)).astype(BF16)
        high = high + lax.dot_general(top, at, NT, preferred_element_type=F32)
        low = low + lax.dot_general(rest, at, NT, preferred_element_type=F32)
    req[:, 0, :] = (high * 32.0 + low).astype(I32)

    def ask(k, carry):
        to = lax.rem(me + k, N_DP)
        remote(req.at[to], asked.at[me], req_s, req_r, (to, x)).start()
        return carry

    lax.fori_loop(1, N_DP, ask, 0)
    asked[pl.ds(me, 1)] = req[pl.ds(me, 1)]
    low_table[...] = table_ref[...].astype(BF16)

    some = pl.ds(0, LINE - 1)
    remote(line.at[some], line.at[some], line_s, line_r, sibling).wait()
    weights[core, x * N_Y + y] = line[...].reshape(LINE, F).astype(BF16)

    def block(bx, by):
        return weights.at[core, lax.rem(bx + N_X, N_X) * N_Y + lax.rem(by + N_Y, N_Y)]

    def y_up(s):
        return remote(block(x, y - s), block(x, y - s), up_s.at[s], up_r.at[s], (lax.rem(y + 1, N_Y) * LINE + spot, x))

    def y_dn(s):
        return remote(block(x, y + s), block(x, y + s), dn_s.at[s], dn_r.at[s], (lax.rem(y + N_Y - 1, N_Y) * LINE + spot, x))

    shifts = (0, -1, 1, -2, 2, -3, 3, -4)

    def xp(k):
        return remote(block(x, y + shifts[k]), block(x, y + shifts[k]), xp_s.at[k], xp_r.at[k], (me, lax.rem(x + 1, N_X)))

    def xm(k):
        return remote(block(x, y + shifts[k]), block(x, y + shifts[k]), xm_s.at[k], xm_r.at[k], (me, lax.rem(x + N_X - 1, N_X)))

    def x2(k):
        if k % 2 == 0:
            ref, to = block(x - 1, y + shifts[k]), lax.rem(x + 1, N_X)
        else:
            ref, to = block(x + 1, y + shifts[k]), lax.rem(x + N_X - 1, N_X)
        return remote(ref, ref, x2_s.at[k], x2_r.at[k], (me, to))

    def sib(dx, k):
        ref = block(x + dx, y + shifts[k])
        n = (dx % N_X) * N_Y + k
        return remote(ref, ref, sib_s.at[n], sib_r.at[n], sibling)

    def have(k):
        xp(k).start()
        xm(k).start()
        sib(0, k).start()

    y_up(0).start()
    y_dn(0).start()
    have(0)

    most = pl.ds(0, N_DP - 1)
    remote(req.at[most], asked.at[most], req_s, req_r, sibling).wait()

    def answer(i, carry):
        g = lax.rem(i + me // 4, N_DP // 4)
        ids = jnp.sum(asked[pl.ds(g * 4, 4)], axis=0) - 1
        wide = jnp.transpose(jnp.broadcast_to(ids.astype(F32), (B, B)))
        number = lane.astype(F32)
        pick = jnp.concatenate(
            [jnp.where(wide == number + float(B * k), 1.0, 0.0).astype(BF16) for k in range(OWN // B)], axis=1
        )
        found = jnp.dot(pick, low_table[...], preferred_element_type=F32).astype(BF16)
        snd[pl.ds(g * 4, 4)] = found.reshape(4, SLOTS, E)
        for q in range(4):
            to = g * 4 + q

            @pl.when(to != me)
            def _():
                remote(snd.at[to], ret.at[me], row_s, row_r, (to, x)).start()

            @pl.when(to == me)
            def _():
                ret[pl.ds(me, 1)] = snd[pl.ds(me, 1)]

        return carry

    for s in range(1, 5):
        lax.fori_loop((s - 1) * 8, s * 8, answer, 0)
        y_up(s - 1).wait_recv()
        if s < 4:
            y_up(s).start()
        have(2 * s - 1)
        if s < 4:
            y_dn(s - 1).wait_recv()
            if s < 3:
                y_dn(s).start()
            have(2 * s)

    for k in range(N_Y):
        xp(k).wait_recv()
        if k % 2 == 0:
            x2(k).start()
        sib(-1, k).start()
        xm(k).wait_recv()
        if k % 2 == 1:
            x2(k).start()
        sib(1, k).start()
    for k in range(N_Y):
        x2(k).wait_recv()
        sib(2, k).start()
    remote(snd.at[most], ret.at[most], row_s, row_r, sibling).wait()
    for s in range(4):
        y_up(s).wait_send()
    for s in range(3):
        y_dn(s).wait_send()
    for k in range(N_Y):
        xp(k).wait_send()
        xm(k).wait_send()
        x2(k).wait_send()
    for dx in range(N_X):
        for k in range(N_Y):
            sib(dx, k).wait()


def dense_kernel(
    place, ret, weights, hot_rows, hot_cols, table_ref, labels, bias, gain,
    out_ref, hot_ref,
    rows, x0, cold, upper, pick, split,
):
    rows[...] = ret[...].astype(F32)

    for j in range(NC):

        def fetch(b, carry, j=j):
            cold[pl.ds(j * B + b, 1), :] = rows[pl.ds(place[j, b], 1), :]
            return carry

        lax.fori_loop(0, B, fetch, 0, unroll=16)
    low_table = table_ref[...].astype(BF16)
    number = iota((B, HOT), 1)
    for j in range(NH):
        one = jnp.where(hot_cols[:, j : j + 1] == number, 1.0, 0.0).astype(BF16)
        x0[:, j * E : (j + 1) * E] = jnp.dot(one, low_table, preferred_element_type=F32).astype(BF16)
    for j in range(NC):
        x0[:, (NH + j) * E : (NH + j + 1) * E] = cold[j * B : (j + 1) * B, :].astype(BF16)
    hid = lax.dot_general(x0[...], weights[0], NT, preferred_element_type=F32).astype(BF16)
    logit = jnp.zeros((B, 1), F32)
    wide = 256
    for n in range(F // wide):
        cut = slice(n * wide, (n + 1) * wide)
        u = jnp.dot(hid, weights[1, :, cut], preferred_element_type=F32) + bias[:, cut]
        upper[:, cut] = u
        xf = x0[:, cut].astype(F32)
        logit = logit + jnp.sum((xf * u + xf) * gain[:, cut], axis=1, keepdims=True)
    delta = jax.nn.sigmoid(logit) - labels[...].astype(F32)
    d_hid = jnp.zeros((B, R), F32)
    for n in range(F // wide):
        cut = slice(n * wide, (n + 1) * wide)
        d_up = ((delta * gain[:, cut]) * x0[:, cut].astype(F32)).astype(BF16)
        d_hid = d_hid + lax.dot_general(d_up, weights[1, :, cut], NT, preferred_element_type=F32)
    d_hid = d_hid.astype(BF16)
    for n in range(F // wide):
        cut = slice(n * wide, (n + 1) * wide)
        grad = (delta * gain[:, cut]) * (upper[:, cut] + 1.0) + jnp.dot(
            d_hid, weights[0, :, cut], preferred_element_type=F32
        )
        for half in range(2):
            j = 2 * n + half
            part = grad[:, half * E : (half + 1) * E]
            if j < NH:
                first = part.astype(BF16)
                split[j * B : (j + 1) * B, :E] = first
                split[j * B : (j + 1) * B, E:] = (part - first.astype(F32)).astype(BF16)
            else:
                cold[(j - NH) * B : (j - NH + 1) * B, :] = part
    height = iota((HOT, B), 0)
    for j in range(NH):
        pick[:, j * B : (j + 1) * B] = jnp.where(height == hot_rows[j : j + 1, :], 1.0, 0.0).astype(BF16)
    both = jnp.dot(pick[...], split[...], preferred_element_type=F32)
    hot_ref[...] = both[:, :E] + both[:, E:]

    for j in range(NC):

        def put(b, carry, j=j):
            rows[pl.ds(place[j, b], 1), :] = cold[pl.ds(j * B + b, 1), :]
            return carry

        lax.fori_loop(0, B, put, 0, unroll=16)
    out_ref[...] = rows[...].astype(BF16)


def compensate(table, backup, grad, rate):
    step_size = rate * grad
    return table - step_size - 0.5 * step_size * step_size * (table - backup.astype(F32))


def update_kernel(
    rate_hot, rate_cold,
    outgoing, asked, hot_part, hot_table, hot_backup, cold_table, cold_backup,
    new_hot, new_cold,
    inc, from_core, mine, from_x, line_sum, from_z, tiny, from_y, part, from_part,
    inc_s, inc_r, hs, hr, gs, gr, ps, pr, as_, ar,
):
    me = lax.axis_index("dp")
    x = lax.axis_index("rep")
    y = me // LINE
    spot = lax.rem(me, LINE)
    z = spot // 2
    core = lax.rem(me, 2)
    sibling = (me + 1 - 2 * core, x)
    enter(me, x, (1, 2, 3))

    half, quarter, thin = HOT // 2, HOT // 8, HOT // 64

    swap = remote(hot_part.at[pl.ds((1 - core) * half, half)], from_core, hs.at[0], hr.at[0], sibling)
    swap.start()

    def give(k, carry):
        to = lax.rem(me + k, N_DP)
        remote(outgoing.at[to], inc.at[me], inc_s, inc_r, (to, x)).start()
        return carry

    lax.fori_loop(1, N_DP, give, 0)
    inc[pl.ds(me, 1)] = outgoing[pl.ds(me, 1)]

    swap.wait()
    mine[...] = hot_part[pl.ds(core * half, half), :] + from_core[...]
    for d in range(1, N_X):
        to = lax.rem(x + d, N_X)
        remote(mine.at[pl.ds(to * quarter, quarter)], from_x.at[x], hs.at[1], hr.at[1], (me, to)).start()
    from_x[pl.ds(x, 1)] = mine[pl.ds(x * quarter, quarter), :].reshape(1, quarter, E)
    remote(from_x.at[pl.ds(0, N_X - 1)], from_x.at[pl.ds(0, N_X - 1)], hs.at[1], hr.at[1], sibling).wait()
    line_sum[...] = (from_x[0] + from_x[1]) + (from_x[2] + from_x[3])
    for d in range(1, N_Z):
        to = lax.rem(z + d, N_Z)
        remote(
            line_sum.at[pl.ds(to * thin, thin)], from_z.at[z], hs.at[2], hr.at[2], (y * LINE + to * 2 + core, x)
        ).start()
    from_z[pl.ds(z, 1)] = line_sum[pl.ds(z * thin, thin), :].reshape(1, thin, E)
    remote(from_z.at[pl.ds(0, N_Z - 1)], from_z.at[pl.ds(0, N_Z - 1)], hs.at[2], hr.at[2], sibling).wait()
    tiny[...] = jnp.sum(from_z[...], axis=0)
    for d in range(1, N_Y):
        to = lax.rem(y + d, N_Y)
        remote(tiny, from_y.at[y], hs.at[3], hr.at[3], (to * LINE + spot, x)).start()
    from_y[pl.ds(y, 1)] = tiny[...].reshape(1, thin, E)
    remote(from_y.at[pl.ds(0, N_Y - 1)], from_y.at[pl.ds(0, N_Y - 1)], hs.at[3], hr.at[3], sibling).wait()
    total = jnp.sum(from_y[...], axis=0)
    base = core * half + x * quarter + z * thin
    spot_rows = pl.ds(pl.multiple_of(base, thin), thin)
    new_hot[spot_rows, :] = compensate(hot_table[spot_rows, :], hot_backup[spot_rows, :], total, rate_hot)
    for d in range(1, N_Z):
        to = lax.rem(z + d, N_Z)
        remote(
            new_hot.at[spot_rows], new_hot.at[spot_rows], hs.at[4], hr.at[4], (y * LINE + to * 2 + core, x)
        ).start()

    most = pl.ds(0, N_DP - 1)
    remote(outgoing.at[most], inc.at[most], inc_s, inc_r, sibling).wait()
    chunk = OWN // N_X

    def sum_rows(which):
        height = iota((chunk, B), 0) + which * chunk

        def add(g, total):
            ids = [jnp.sum(asked[pl.ds(g * 8 + 4 * q, 4)], axis=0) - 1 for q in range(2)]
            pick = jnp.concatenate([jnp.where(height == i, 1.0, 0.0).astype(BF16) for i in ids], axis=1)
            return total + jnp.dot(pick, inc[pl.ds(g * 8, 8)].reshape(8 * SLOTS, E), preferred_element_type=F32)

        return lax.fori_loop(0, N_DP // 8, add, jnp.zeros((chunk, E), F32))

    def send_part(d):
        return remote(part.at[d - 1], from_part.at[d - 1], ps.at[d - 1], pr.at[d - 1], (me, lax.rem(x + d, N_X)))

    for d in (2, 1, 3):
        part[d - 1] = sum_rows(lax.rem(x + d, N_X)).astype(BF16)
        send_part(d).start()
    remote(
        new_hot.at[pl.ds(0, (N_Z - 1) * thin)], new_hot.at[pl.ds(0, (N_Z - 1) * thin)], hs.at[4], hr.at[4], sibling
    ).wait()
    x_rows = pl.ds(pl.multiple_of(core * half + x * quarter, quarter), quarter)
    for d in range(1, N_X):
        to = lax.rem(x + d, N_X)
        remote(new_hot.at[x_rows], new_hot.at[x_rows], gs.at[0], gr.at[0], (me, to)).start()
    cold = sum_rows(x)
    remote(
        new_hot.at[pl.ds(0, (N_X - 1) * quarter)], new_hot.at[pl.ds(0, (N_X - 1) * quarter)], gs.at[0], gr.at[0], sibling
    ).wait()
    core_rows = pl.ds(pl.multiple_of(core * half, half), half)
    last = remote(new_hot.at[core_rows], new_hot.at[core_rows], gs.at[1], gr.at[1], sibling)
    last.start()
    for d in (2, 1, 3):
        send_part(d).wait()
        cold = cold + from_part[d - 1].astype(F32)

    def cold_rows(dx, start, size):
        first = lax.rem(x + dx + N_X, N_X) * chunk + start
        return pl.ds(pl.multiple_of(first, size), size)

    own = cold_rows(0, 0, chunk)
    new_cold[own, :] = compensate(cold_table[own, :], cold_backup[own, :], cold, rate_cold)

    def pass_on(n, rows, step):
        return remote(new_cold.at[rows], new_cold.at[rows], as_.at[n], ar.at[n], (me, lax.rem(x + step, N_X)))

    right = pass_on(0, own, 1)
    left = pass_on(1, own, N_X - 1)
    right.start()
    left.start()
    right.wait_recv()
    right2 = pass_on(2, cold_rows(-1, 0, chunk // 2), 1)
    right2.start()
    left.wait_recv()
    left2 = pass_on(3, cold_rows(1, chunk // 2, chunk // 2), N_X - 1)
    left2.start()
    right.wait_send()
    left.wait_send()
    right2.wait()
    left2.wait()
    last.wait()


VMEM = pl.BlockSpec(memory_space=pltpu.VMEM)
SMEM = pl.BlockSpec(memory_space=pltpu.SMEM)
DMA = pltpu.SemaphoreType.DMA


def shards(
    hot_ids, cold_rows, cold_owner, labels, hot_table, hot_backup,
    cold_table, cold_backup, cross_down, cross_up, cross_bias, out_weight,
):
    rows = hot_ids.shape[0]
    n_data = lax.axis_size("dp")
    n_reps = lax.axis_size("rep")
    batch_all = rows * n_data * n_reps
    rate_hot = 20.0 * math.sqrt(HOT / (batch_all * NH))
    rate_cold = 20.0 * math.sqrt(OWN * n_data / (batch_all * NC))

    owner = cold_owner.reshape(B, NC).T
    shard = jnp.stack([cross_down.reshape(1, F), cross_up.reshape(1, F)]).astype(F32)
    ret, weights, asked, place = pl.pallas_call(
        fetch_kernel,
        out_shape=(
            jax.ShapeDtypeStruct((N_DP, SLOTS, E), BF16),
            jax.ShapeDtypeStruct((2, N_X * N_Y, LINE, F), BF16),
            jax.ShapeDtypeStruct((N_DP, 1, B), I32),
            jax.ShapeDtypeStruct((NC, B), I32),
        ),
        in_specs=[VMEM] * 4,
        out_specs=[VMEM] * 4,
        scratch_shapes=[
            pltpu.VMEM((N_DP, 1, B), I32),
            pltpu.VMEM((OWN, E), BF16),
            pltpu.VMEM((N_DP, SLOTS, E), BF16),
            pltpu.VMEM((LINE, 1, F), F32),
            DMA, DMA, DMA, DMA, DMA, DMA,
            DMA((4,)), DMA((4,)), DMA((3,)), DMA((3,)),
            DMA((8,)), DMA((8,)), DMA((8,)), DMA((8,)), DMA((8,)), DMA((8,)), DMA((32,)), DMA((32,)),
        ],
        compiler_params=pltpu.CompilerParams(
            collective_id=0, has_side_effects=True, vmem_limit_bytes=40 << 20
        ),
        name="fetch",
    )(owner, cold_rows.T, shard, cold_table)

    outgoing, hot_part = pl.pallas_call(
        dense_kernel,
        out_shape=(
            jax.ShapeDtypeStruct((N_DP * SLOTS, E), BF16),
            jax.ShapeDtypeStruct((HOT, E), F32),
        ),
        in_specs=[SMEM] + [VMEM] * 8,
        out_specs=[VMEM] * 2,
        scratch_shapes=[
            pltpu.VMEM((N_DP * SLOTS, E), F32),
            pltpu.VMEM((B, F), BF16),
            pltpu.VMEM((NC * B, E), F32),
            pltpu.VMEM((B, F), F32),
            pltpu.VMEM((HOT, NH * B), BF16),
            pltpu.VMEM((NH * B, 2 * E), BF16),
        ],
        compiler_params=pltpu.CompilerParams(vmem_limit_bytes=48 << 20),
        name="dense",
    )(
        place, ret.reshape(N_DP * SLOTS, E), weights.reshape(2, R, F), hot_ids.T, hot_ids, hot_table,
        labels.reshape(B, 1), cross_bias.reshape(1, F), out_weight.reshape(1, F),
    )

    def update(*refs):
        update_kernel(rate_hot, rate_cold, *refs)

    new_hot, new_cold = pl.pallas_call(
        update,
        out_shape=(
            jax.ShapeDtypeStruct((HOT, E), F32),
            jax.ShapeDtypeStruct((OWN, E), F32),
        ),
        in_specs=[VMEM] * 7,
        out_specs=[VMEM] * 2,
        scratch_shapes=[
            pltpu.VMEM((N_DP, SLOTS, E), BF16),
            pltpu.VMEM((HOT // 2, E), F32),
            pltpu.VMEM((HOT // 2, E), F32),
            pltpu.VMEM((N_X, HOT // 8, E), F32),
            pltpu.VMEM((HOT // 8, E), F32),
            pltpu.VMEM((N_Z, HOT // 64, E), F32),
            pltpu.VMEM((HOT // 64, E), F32),
            pltpu.VMEM((N_Y, HOT // 64, E), F32),
            pltpu.VMEM((3, OWN // N_X, E), BF16),
            pltpu.VMEM((3, OWN // N_X, E), BF16),
            DMA, DMA, DMA((5,)), DMA((5,)), DMA((2,)), DMA((2,)),
            DMA((3,)), DMA((3,)), DMA((4,)), DMA((4,)),
        ],
        compiler_params=pltpu.CompilerParams(
            collective_id=1, has_side_effects=True, vmem_limit_bytes=40 << 20
        ),
        name="update",
    )(outgoing.reshape(N_DP, SLOTS, E), asked, hot_part, hot_table, hot_backup, cold_table, cold_backup)
    return (new_hot, new_cold)


def solution(mesh):
    placed = (
        P(("dp", "rep"), None),
        P(("dp", "rep"), None),
        P(("dp", "rep"), None),
        P(("dp", "rep")),
        P(),
        P(),
        P("dp", None),
        P("dp", None),
        P(None, ("dp", "rep")),
        P(("dp", "rep"), None),
        P(),
        P(),
    )
    return jax.shard_map(
        shards, mesh=mesh, in_specs=placed, out_specs=(P(), P("dp", None)), check_vma=False
    )
```

```python
import math

import jax
import jax.numpy as jnp
from jax import lax
from jax.experimental import pallas as pl
from jax.experimental.pallas import tpu as pltpu
from jax.sharding import PartitionSpec as P

E = 128
NH = 13
NC = 13
HOT = 1024
F = 3328
R = 512
B = 128
OWN = 2048
SLOTS = 32
CAP = 26
PAIRS = CAP // 2
PAD = 8
SHIFT = 53
UNSHIFT = 29
N_DP = 128
N_X = 4
N_Y = 8
N_Z = 8
LINE = 2 * N_Z
MESH = pl.DeviceIdType.MESH
F32 = jnp.float32
BF16 = jnp.bfloat16
I32 = jnp.int32

NT = (((1,), (1,)), ((), ()))


def remote(src, dst, send, recv, device):
    return pltpu.make_async_remote_copy(
        src_ref=src, dst_ref=dst, send_sem=send, recv_sem=recv, device_id=device, device_id_type=MESH
    )


def iota(shape, dim):
    return lax.broadcasted_iota(I32, shape, dim)


def enter_signal(barrier, me, x):
    def greet(k, carry):
        pl.semaphore_signal(barrier, inc=1, device_id=(lax.rem(me + k, N_DP), x), device_id_type=MESH)
        return carry

    lax.fori_loop(1, N_DP, greet, 0)
    for step in range(1, N_X):
        pl.semaphore_signal(barrier, inc=1, device_id=(me, lax.rem(x + step, N_X)), device_id_type=MESH)


def compensate(table, backup, grad, rate):
    step_size = rate * grad
    return table - step_size - 0.5 * step_size * step_size * (table - backup.astype(F32))


def step_kernel(
    rate_hot, rate_cold,
    owner_ref, rows_ref, shard_ref, hot_rows, labels, affine,
    cold_hbm, cold_backup_hbm, hot_hbm, hot_backup_hbm,
    new_hot, new_cold,
    cold_backup, hot_table, hot_backup, table,
    req, asked, place, inverse, ask_s, place_s, inverse_s,
    snd, ret, inc, line, weights,
    rows, x0, cold, upper, pick, split, hot_part, acc,
    from_core, mine, from_x, line_sum, from_z, tiny, from_y, part, from_part,
    load, req_s, req_r, row_s, row_r, line_s, line_r,
    up_s, up_r, dn_s, dn_r, xp_s, xp_r, xm_s, xm_r, x2_s, x2_r, sib_s, sib_r,
    inc_s, inc_r, hs, hr, gs, gr, ps, pr, as_, ar,
):
    me = lax.axis_index("dp")
    x = lax.axis_index("rep")
    y = me // LINE
    spot = lax.rem(me, LINE)
    z = spot // 2
    core = lax.rem(me, 2)
    sibling = (me + 1 - 2 * core, x)

    barrier = pltpu.get_barrier_semaphore()
    enter_signal(barrier, me, x)
    loads = [
        pltpu.make_async_copy(cold_hbm, table.at[pl.ds(PAD, OWN)], load.at[0]),
        pltpu.make_async_copy(hot_hbm, hot_table, load.at[1]),
        pltpu.make_async_copy(hot_backup_hbm, hot_backup, load.at[2]),
        pltpu.make_async_copy(cold_backup_hbm, cold_backup, load.at[3]),
    ]
    for copy in loads:
        copy.start()
    table[pl.ds(0, PAD), :] = jnp.zeros((PAD, E), F32)
    cold[pl.ds(0, PAD), :] = jnp.zeros((PAD, E), F32)
    inc[:, PAIRS:] = jnp.zeros((N_DP, SLOTS // 2 - PAIRS, 2, E), BF16)

    sub = iota((B, B), 0)
    lane = iota((B, B), 1)
    lane_row = iota((1, B), 1)
    before = jnp.where(sub < lane, 1.0, 0.0).astype(BF16)
    count = jnp.zeros((N_DP, 1), F32)
    codes = jnp.zeros((4 * N_DP, B), F32)
    for j in range(NC):
        spot_n = ((owner_ref[j : j + 1, :] - me + N_DP) * UNSHIFT) & (N_DP - 1)
        hit = jnp.where(sub == spot_n, 1.0, 0.0)
        rank = jnp.dot(hit.astype(BF16), before, preferred_element_type=F32) + count
        slot = jnp.sum(hit * rank, axis=0, keepdims=True).astype(I32)
        count = count + jnp.sum(hit, axis=1, keepdims=True)
        place[j : j + 1, :] = spot_n * SLOTS + jnp.clip(slot, 0, CAP - 1)
        at = jnp.where(sub == slot + SLOTS * (spot_n & 3), 1.0, 0.0).astype(BF16)
        row = rows_ref[j : j + 1, :] + PAD
        number = lane_row + (j * B + PAD)
        parts = [(hit * v.astype(F32)).astype(BF16) for v in (row >> 5, row & 31, number >> 5, number & 31)]
        codes = codes + lax.dot_general(jnp.concatenate(parts, axis=0), at, NT, preferred_element_type=F32)
    req[:, 0, :] = jnp.clip((codes[:N_DP] * 32.0 + codes[N_DP : 2 * N_DP]).astype(I32), 0, OWN + PAD - 1)
    inverse[...] = jnp.clip((codes[2 * N_DP : 3 * N_DP] * 32.0 + codes[3 * N_DP :]).astype(I32), 0, NC * B + PAD - 1)
    pl.semaphore_wait(barrier, N_DP + N_X - 2)

    def line_send(k, carry):
        to = lax.rem(spot + k, LINE)
        remote(shard_ref.at[lax.rem(to, 2)], line.at[spot], line_s, line_r, (y * LINE + to, x)).start()
        return carry

    lax.fori_loop(1, LINE, line_send, 0)
    line[pl.ds(spot, 1)] = shard_ref[pl.ds(core, 1)]

    def ask(n, carry):
        to = lax.rem(me + n * SHIFT, N_DP)
        remote(req.at[n], asked.at[n], req_s, req_r, (to, x)).start()
        return carry

    lax.fori_loop(1, N_DP, ask, 0)
    asked[0] = req[0]
    place_copy = pltpu.make_async_copy(place, place_s, load.at[4])
    place_copy.start()
    inverse_copy = pltpu.make_async_copy(inverse, inverse_s, load.at[5])
    inverse_copy.start()

    some = pl.ds(0, LINE - 1)
    remote(line.at[some], line.at[some], line_s, line_r, sibling).wait()
    weights[core, x * N_Y + y] = line[...].reshape(LINE, F).astype(BF16)

    def block(bx, by):
        return weights.at[core, lax.rem(bx + N_X, N_X) * N_Y + lax.rem(by + N_Y, N_Y)]

    def y_up(s):
        return remote(block(x, y - s), block(x, y - s), up_s.at[s], up_r.at[s], (lax.rem(y + 1, N_Y) * LINE + spot, x))

    def y_dn(s):
        return remote(block(x, y + s), block(x, y + s), dn_s.at[s], dn_r.at[s], (lax.rem(y + N_Y - 1, N_Y) * LINE + spot, x))

    shifts = (0, -1, 1, -2, 2, -3, 3, -4)

    def xp(k):
        return remote(block(x, y + shifts[k]), block(x, y + shifts[k]), xp_s.at[k], xp_r.at[k], (me, lax.rem(x + 1, N_X)))

    def xm(k):
        return remote(block(x, y + shifts[k]), block(x, y + shifts[k]), xm_s.at[k], xm_r.at[k], (me, lax.rem(x + N_X - 1, N_X)))

    def x2(k):
        if k % 2 == 0:
            ref, to = block(x - 1, y + shifts[k]), lax.rem(x + 1, N_X)
        else:
            ref, to = block(x + 1, y + shifts[k]), lax.rem(x + N_X - 1, N_X)
        return remote(ref, ref, x2_s.at[k], x2_r.at[k], (me, to))

    def sib(dx, k):
        ref = block(x + dx, y + shifts[k])
        n = (dx % N_X) * N_Y + k
        return remote(ref, ref, sib_s.at[n], sib_r.at[n], sibling)

    def have(k):
        xp(k).start()
        xm(k).start()
        sib(0, k).start()

    y_up(0).start()
    y_dn(0).start()
    have(0)

    most = pl.ds(0, N_DP - 1)
    remote(req.at[most], asked.at[most], req_s, req_r, sibling).wait()
    ask_copy = pltpu.make_async_copy(asked, ask_s, load.at[6])
    ask_copy.start()
    loads[0].wait()
    ask_copy.wait()
    sent = pl.ds(0, PAIRS)

    def gather(n, source, index):
        last = source.shape[0] - 1
        picked = [source[pl.ds(jnp.clip(index(i), 0, last), 1), :] for i in range(CAP)]
        full = jnp.concatenate(picked + [jnp.zeros((SLOTS - CAP, E), F32)], axis=0)
        snd[pl.ds(n, 1)] = full.astype(BF16).reshape(1, SLOTS // 2, 2, E)

    def answer(n, carry):
        corner = lax.rem(n, 4) * SLOTS
        gather(n, table, lambda i: ask_s[n, 0, corner + i])
        to = lax.rem(me + n * (N_DP - SHIFT), N_DP)
        remote(snd.at[n, sent], ret.at[n, sent], row_s, row_r, (to, x)).start()
        return carry

    for s in range(1, 5):
        lax.fori_loop(max(1, (s - 1) * 32), s * 32, answer, 0)
        y_up(s - 1).wait_recv()
        if s < 4:
            y_up(s).start()
        have(2 * s - 1)
        if s < 4:
            y_dn(s - 1).wait_recv()
            if s < 3:
                y_dn(s).start()
            have(2 * s)

    loads[1].wait()
    low_table = hot_table[...].astype(BF16)
    number = iota((B, HOT), 1).astype(F32)
    height = iota((HOT, B), 0)

    def hot_slot(j):
        ids = hot_rows[j : j + 1, :]
        column = jnp.transpose(jnp.broadcast_to(ids.astype(F32), (B, B)))
        wide = jnp.concatenate([column] * (HOT // B), axis=1)
        one = jnp.where(wide == number, 1.0, 0.0).astype(BF16)
        x0[:, j * E : (j + 1) * E] = jnp.dot(one, low_table, preferred_element_type=F32).astype(BF16)
        pick[:, j * B : (j + 1) * B] = jnp.where(height == ids, 1.0, 0.0).astype(BF16)

    for k in range(N_Y):
        xp(k).wait_recv()
        if k % 2 == 0:
            x2(k).start()
        sib(-1, k).start()
        xm(k).wait_recv()
        if k % 2 == 1:
            x2(k).start()
        sib(1, k).start()
        hot_slot(k)
    for j in range(N_Y, NH):
        hot_slot(j)

    gather(0, table, lambda i: ask_s[0, 0, i])
    ret[0, sent] = snd[0, sent]
    remote(snd.at[most, sent], ret.at[most, sent], row_s, row_r, sibling).wait()
    rows[...] = ret[...].reshape(N_DP * SLOTS, E).astype(F32)
    place_copy.wait()
    inverse_copy.wait()
    for j in range(NC):

        def fetch(b, carry, j=j):
            at = jnp.clip(place_s[j, b], 0, N_DP * SLOTS - 1)
            cold[pl.ds(PAD + j * B + b, 1), :] = rows[pl.ds(at, 1), :]
            return carry

        lax.fori_loop(0, B, fetch, 0, unroll=16)
    for j in range(NC):
        x0[:, (NH + j) * E : (NH + j + 1) * E] = cold[PAD + j * B : PAD + (j + 1) * B, :].astype(BF16)

    for k in range(N_Y):
        x2(k).wait_recv()
        sib(2, k).start()
    for s in range(4):
        y_up(s).wait_send()
    for s in range(3):
        y_dn(s).wait_send()
    for k in range(N_Y):
        xp(k).wait_send()
        xm(k).wait_send()
        x2(k).wait_send()
    for dx in range(N_X):
        for k in range(N_Y):
            sib(dx, k).wait()

    bias = affine[0:1, :]
    gain = affine[1:2, :]
    down = weights.at[0]
    above = weights.at[1]
    hid = lax.dot_general(x0[...], down[...].reshape(R, F), NT, preferred_element_type=F32).astype(BF16)
    logit = jnp.zeros((B, 1), F32)
    wide = 256
    for n in range(F // wide):
        cut = slice(n * wide, (n + 1) * wide)
        u = jnp.dot(hid, above[:, :, cut].reshape(R, wide), preferred_element_type=F32) + bias[:, cut]
        upper[:, cut] = u
        xf = x0[:, cut].astype(F32)
        logit = logit + jnp.sum((xf * u + xf) * gain[:, cut], axis=1, keepdims=True)
    label = jnp.transpose(jnp.broadcast_to(labels[...].astype(F32), (B, B)))[:, 0:1]
    delta = jax.nn.sigmoid(logit) - label
    d_hid = jnp.zeros((B, R), F32)
    for n in range(F // wide):
        cut = slice(n * wide, (n + 1) * wide)
        d_up = ((delta * gain[:, cut]) * x0[:, cut].astype(F32)).astype(BF16)
        d_hid = d_hid + lax.dot_general(d_up, above[:, :, cut].reshape(R, wide), NT, preferred_element_type=F32)
    d_hid = d_hid.astype(BF16)

    def slots(n):
        cut = slice(n * wide, (n + 1) * wide)
        grad = (delta * gain[:, cut]) * (upper[:, cut] + 1.0) + jnp.dot(
            d_hid, down[:, :, cut].reshape(R, wide), preferred_element_type=F32
        )
        for half in range(2):
            j = 2 * n + half
            value = grad[:, half * E : (half + 1) * E]
            if j < NH:
                first = value.astype(BF16)
                split[j * B : (j + 1) * B, :E] = first
                split[j * B : (j + 1) * B, E:] = (value - first.astype(F32)).astype(BF16)
            else:
                cold[PAD + (j - NH) * B : PAD + (j - NH + 1) * B, :] = value

    for n in reversed(range(NH // 2, F // wide)):
        slots(n)

    def give(n, carry):
        corner = lax.rem(n, 4) * SLOTS
        gather(n, cold, lambda i: inverse_s[n, corner + i])
        to = lax.rem(me + n * SHIFT, N_DP)
        batch = n // 32
        remote(snd.at[n, sent], inc.at[n, sent], inc_s.at[batch], inc_r.at[batch], (to, x)).start()
        return carry

    lax.fori_loop(1, N_DP, give, 0)
    gather(0, cold, lambda i: inverse_s[0, i])
    inc[0, sent] = snd[0, sent]

    for n in range(NH // 2):
        slots(n)
    both = jnp.dot(pick[...], split[...], preferred_element_type=F32)
    hot_part[...] = both[:, :E] + both[:, E:]
    half, quarter, thin = HOT // 2, HOT // 8, HOT // 64
    swap = remote(hot_part.at[pl.ds((1 - core) * half, half)], from_core, hs.at[0], hr.at[0], sibling)
    swap.start()

    one, zero = jnp.ones((), BF16), jnp.zeros((), BF16)
    chunk = OWN // N_X

    def batch_ids(b):
        ids = [jnp.sum(asked[pl.ds(b * 32 + 4 * q, 4)], axis=0) - PAD for q in range(8)]
        return jnp.concatenate(ids, axis=1).astype(F32)

    def batch_sum(ids, b, first):
        tall = iota((256, B), 0).astype(F32).astype(BF16)
        halves = []
        for r in range(chunk // 256):
            near = (ids - (first + 256 * r).astype(F32)).astype(BF16)
            halves.append(
                jnp.concatenate(
                    [jnp.where(tall == near[:, q * B : (q + 1) * B], one, zero) for q in range(8)], axis=1
                )
            )
        values = inc[b * 32 : (b + 1) * 32].reshape(32 * SLOTS, E)
        return jnp.dot(jnp.concatenate(halves, axis=0), values, preferred_element_type=F32)

    def batch_wait(b):
        got = pl.ds(32 * b, 32) if b else pl.ds(1, 31)
        remote(snd.at[got, sent], inc.at[got, sent], inc_s.at[b], inc_r.at[b], sibling).wait()

    def batch(b):
        batch_wait(b)
        ids = batch_ids(b)

        def add(c, carry):
            here = pl.ds(pl.multiple_of(c * chunk, chunk), chunk)
            value = batch_sum(ids, b, c * chunk)
            acc[here, :] = value if b == 0 else acc[here, :] + value
            return carry

        lax.fori_loop(0, N_X, add, 0)

    swap.wait()
    mine[...] = hot_part[pl.ds(pl.multiple_of(core * half, half), half), :] + from_core[...]
    for d in range(1, N_X):
        to = lax.rem(x + d, N_X)
        remote(mine.at[pl.ds(to * quarter, quarter)], from_x.at[x], hs.at[1], hr.at[1], (me, to)).start()
    from_x[pl.ds(x, 1)] = mine[pl.ds(x * quarter, quarter), :].reshape(1, quarter, E)
    batch(0)
    remote(from_x.at[pl.ds(0, N_X - 1)], from_x.at[pl.ds(0, N_X - 1)], hs.at[1], hr.at[1], sibling).wait()
    line_sum[...] = (from_x[0] + from_x[1]) + (from_x[2] + from_x[3])
    for d in range(1, N_Z):
        to = lax.rem(z + d, N_Z)
        remote(
            line_sum.at[pl.ds(to * thin, thin)], from_z.at[z], hs.at[2], hr.at[2], (y * LINE + to * 2 + core, x)
        ).start()
    from_z[pl.ds(z, 1)] = line_sum[pl.ds(z * thin, thin), :].reshape(1, thin, E)
    batch(1)
    remote(from_z.at[pl.ds(0, N_Z - 1)], from_z.at[pl.ds(0, N_Z - 1)], hs.at[2], hr.at[2], sibling).wait()
    tiny[...] = jnp.sum(from_z[...], axis=0)
    for d in range(1, N_Y):
        to = lax.rem(y + d, N_Y)
        remote(tiny, from_y.at[y], hs.at[3], hr.at[3], (to * LINE + spot, x)).start()
    from_y[pl.ds(y, 1)] = tiny[...].reshape(1, thin, E)
    batch(2)
    remote(from_y.at[pl.ds(0, N_Y - 1)], from_y.at[pl.ds(0, N_Y - 1)], hs.at[3], hr.at[3], sibling).wait()
    total = jnp.sum(from_y[...], axis=0)
    base = core * half + x * quarter + z * thin
    spot_rows = pl.ds(pl.multiple_of(base, thin), thin)
    loads[2].wait()
    loads[3].wait()
    new_hot[spot_rows, :] = compensate(hot_table[spot_rows, :], hot_backup[spot_rows, :], total, rate_hot)
    for d in range(1, N_Z):
        to = lax.rem(z + d, N_Z)
        remote(
            new_hot.at[spot_rows], new_hot.at[spot_rows], hs.at[4], hr.at[4], (y * LINE + to * 2 + core, x)
        ).start()

    def send_part(d):
        return remote(part.at[d - 1], from_part.at[d - 1], ps.at[d - 1], pr.at[d - 1], (me, lax.rem(x + d, N_X)))

    batch_wait(3)
    ids = batch_ids(3)

    def finish(d):
        which = lax.rem(x + d, N_X) * chunk
        return acc[pl.ds(pl.multiple_of(which, chunk), chunk), :] + batch_sum(ids, 3, which)

    for d in (2, 1, 3):
        part[d - 1] = finish(d).astype(BF16)
        send_part(d).start()
    total_cold = finish(0)
    remote(
        new_hot.at[pl.ds(0, (N_Z - 1) * thin)], new_hot.at[pl.ds(0, (N_Z - 1) * thin)], hs.at[4], hr.at[4], sibling
    ).wait()
    x_rows = pl.ds(pl.multiple_of(core * half + x * quarter, quarter), quarter)
    for d in range(1, N_X):
        to = lax.rem(x + d, N_X)
        remote(new_hot.at[x_rows], new_hot.at[x_rows], gs.at[0], gr.at[0], (me, to)).start()
    for d in (2, 1, 3):
        send_part(d).wait()
        total_cold = total_cold + from_part[d - 1].astype(F32)

    def cold_rows(dx, start, size):
        first = lax.rem(x + dx + N_X, N_X) * chunk + start
        return pl.ds(pl.multiple_of(first, size), size)

    own = cold_rows(0, 0, chunk)
    own_table = table[pl.ds(pl.multiple_of(x * chunk + PAD, PAD), chunk), :]
    new_cold[own, :] = compensate(own_table, cold_backup[own, :], total_cold, rate_cold)

    def pass_on(n, span, step):
        return remote(new_cold.at[span], new_cold.at[span], as_.at[n], ar.at[n], (me, lax.rem(x + step, N_X)))

    right = pass_on(0, own, 1)
    left = pass_on(1, own, N_X - 1)
    right.start()
    left.start()
    remote(
        new_hot.at[pl.ds(0, (N_X - 1) * quarter)], new_hot.at[pl.ds(0, (N_X - 1) * quarter)], gs.at[0], gr.at[0], sibling
    ).wait()
    core_rows = pl.ds(pl.multiple_of(core * half, half), half)
    last = remote(new_hot.at[core_rows], new_hot.at[core_rows], gs.at[1], gr.at[1], sibling)
    last.start()
    right.wait_recv()
    right2 = pass_on(2, cold_rows(-1, 0, chunk // 2), 1)
    right2.start()
    left.wait_recv()
    left2 = pass_on(3, cold_rows(1, chunk // 2, chunk // 2), N_X - 1)
    left2.start()
    right.wait_send()
    left.wait_send()
    right2.wait()
    left2.wait()
    last.wait()


VMEM = pl.BlockSpec(memory_space=pltpu.VMEM)
ANY = pl.BlockSpec(memory_space=pl.ANY)
DMA = pltpu.SemaphoreType.DMA


def shards(
    hot_ids, cold_rows, cold_owner, labels, hot_table, hot_backup,
    cold_table, cold_backup, cross_down, cross_up, cross_bias, out_weight,
):
    rows = hot_ids.shape[0]
    n_data = lax.axis_size("dp")
    n_reps = lax.axis_size("rep")
    batch_all = rows * n_data * n_reps
    rate_hot = 20.0 * math.sqrt(HOT / (batch_all * NH))
    rate_cold = 20.0 * math.sqrt(OWN * n_data / (batch_all * NC))

    owner = cold_owner.reshape(B, NC).T
    shard = jnp.stack([cross_down.reshape(1, F), cross_up.reshape(1, F)]).astype(F32)
    affine = jnp.stack([cross_bias, out_weight])

    def kernel(*refs):
        step_kernel(rate_hot, rate_cold, *refs)

    return pl.pallas_call(
        kernel,
        out_shape=(
            jax.ShapeDtypeStruct((HOT, E), F32),
            jax.ShapeDtypeStruct((OWN, E), F32),
        ),
        in_specs=[VMEM] * 6 + [ANY] * 4,
        out_specs=(VMEM, VMEM),
        scratch_shapes=[
            pltpu.VMEM((OWN, E), BF16),
            pltpu.VMEM((HOT, E), F32),
            pltpu.VMEM((HOT, E), BF16),
            pltpu.VMEM((OWN + PAD, E), F32),
            pltpu.VMEM((N_DP, 1, B), I32),
            pltpu.VMEM((N_DP, 1, B), I32),
            pltpu.VMEM((NC, B), I32),
            pltpu.VMEM((N_DP, B), I32),
            pltpu.SMEM((N_DP, 1, B), I32),
            pltpu.SMEM((NC, B), I32),
            pltpu.SMEM((N_DP, B), I32),
            pltpu.VMEM((N_DP, SLOTS // 2, 2, E), BF16),
            pltpu.VMEM((N_DP, SLOTS // 2, 2, E), BF16),
            pltpu.VMEM((N_DP, SLOTS // 2, 2, E), BF16),
            pltpu.VMEM((LINE, 1, F), F32),
            pltpu.VMEM((2, N_X * N_Y, LINE, F), BF16),
            pltpu.VMEM((N_DP * SLOTS, E), F32),
            pltpu.VMEM((B, F), BF16),
            pltpu.VMEM((NC * B + PAD, E), F32),
            pltpu.VMEM((B, F), F32),
            pltpu.VMEM((HOT, NH * B), BF16),
            pltpu.VMEM((NH * B, 2 * E), BF16),
            pltpu.VMEM((HOT, E), F32),
            pltpu.VMEM((OWN, E), F32),
            pltpu.VMEM((HOT // 2, E), F32),
            pltpu.VMEM((HOT // 2, E), F32),
            pltpu.VMEM((N_X, HOT // 8, E), F32),
            pltpu.VMEM((HOT // 8, E), F32),
            pltpu.VMEM((N_Z, HOT // 64, E), F32),
            pltpu.VMEM((HOT // 64, E), F32),
            pltpu.VMEM((N_Y, HOT // 64, E), F32),
            pltpu.VMEM((3, OWN // N_X, E), BF16),
            pltpu.VMEM((3, OWN // N_X, E), BF16),
            DMA((7,)), DMA, DMA, DMA, DMA, DMA, DMA,
            DMA((4,)), DMA((4,)), DMA((3,)), DMA((3,)),
            DMA((8,)), DMA((8,)), DMA((8,)), DMA((8,)), DMA((8,)), DMA((8,)), DMA((32,)), DMA((32,)),
            DMA((4,)), DMA((4,)), DMA((5,)), DMA((5,)), DMA((2,)), DMA((2,)),
            DMA((3,)), DMA((3,)), DMA((4,)), DMA((4,)),
        ],
        compiler_params=pltpu.CompilerParams(
            collective_id=0, has_side_effects=True, vmem_limit_bytes=52 << 20
        ),
        name="step",
    )(
        owner, cold_rows.T, shard, hot_ids.T, labels.reshape(1, B), affine,
        cold_table, cold_backup, hot_table, hot_backup,
    )


def solution(mesh):
    placed = (
        P(("dp", "rep"), None),
        P(("dp", "rep"), None),
        P(("dp", "rep"), None),
        P(("dp", "rep")),
        P(),
        P(),
        P("dp", None),
        P("dp", None),
        P(None, ("dp", "rep")),
        P(("dp", "rep"), None),
        P(),
        P(),
    )
    return jax.shard_map(
        shards, mesh=mesh, in_specs=placed, out_specs=(P(), P("dp", None)), check_vma=False
    )
```

```python
import math

import jax
import jax.numpy as jnp
from jax import lax
from jax.experimental import pallas as pl
from jax.experimental.pallas import tpu as pltpu
from jax.sharding import PartitionSpec as P

E = 128
NH = 13
NC = 13
HOT = 1024
F = 3328
R = 512
B = 128
OWN = 2048
SLOTS = 32
CAP = 26
PAIRS = CAP // 2
PAD = 8
SHIFT = 53
UNSHIFT = 29
N_DP = 128
N_X = 4
N_Y = 8
N_Z = 8
LINE = 2 * N_Z
MESH = pl.DeviceIdType.MESH
F32 = jnp.float32
BF16 = jnp.bfloat16
I32 = jnp.int32

NT = (((1,), (1,)), ((), ()))


def remote(src, dst, send, recv, device):
    return pltpu.make_async_remote_copy(
        src_ref=src, dst_ref=dst, send_sem=send, recv_sem=recv, device_id=device, device_id_type=MESH
    )


def iota(shape, dim):
    return lax.broadcasted_iota(I32, shape, dim)


def enter_signal(barrier, me, x):
    def greet(k, carry):
        pl.semaphore_signal(barrier, inc=1, device_id=(lax.rem(me + k, N_DP), x), device_id_type=MESH)
        return carry

    lax.fori_loop(1, N_DP, greet, 0)
    for step in range(1, N_X):
        pl.semaphore_signal(barrier, inc=1, device_id=(me, lax.rem(x + step, N_X)), device_id_type=MESH)


def compensate(table, backup, grad, rate):
    step_size = rate * grad
    return table - step_size - 0.5 * step_size * step_size * (table - backup.astype(F32))


def step_kernel(
    rate_hot, rate_cold,
    owner_ref, rows_ref, down_ref, up_ref, hot_rows, labels, affine,
    cold_hbm, cold_backup_hbm, hot_hbm, hot_backup_hbm,
    new_hot, new_cold,
    cold_backup, hot_table, hot_backup, table,
    req, asked, place, inverse, ask_s, place_s, inverse_s,
    snd, ret, inc, line, shard_ref, weights,
    rows, x0, cold, upper, pick, split, hot_part, acc,
    from_core, mine, from_x, line_sum, from_z, tiny, from_y, part, from_part,
    load, req_s, req_r, row_s, row_r, line_s, line_r,
    up_s, up_r, dn_s, dn_r, xp_s, xp_r, xm_s, xm_r, x2_s, x2_r, sib_s, sib_r,
    inc_s, inc_r, hs, hr, gs, gr, ps, pr, as_, ar,
):
    me = lax.axis_index("dp")
    x = lax.axis_index("rep")
    y = me // LINE
    spot = lax.rem(me, LINE)
    z = spot // 2
    core = lax.rem(me, 2)
    sibling = (me + 1 - 2 * core, x)

    barrier = pltpu.get_barrier_semaphore()
    enter_signal(barrier, me, x)
    loads = [
        pltpu.make_async_copy(cold_hbm, table.at[pl.ds(PAD, OWN)], load.at[0]),
        pltpu.make_async_copy(hot_hbm, hot_table, load.at[1]),
        pltpu.make_async_copy(hot_backup_hbm, hot_backup, load.at[2]),
        pltpu.make_async_copy(cold_backup_hbm, cold_backup, load.at[3]),
    ]
    for copy in loads:
        copy.start()
    shard_ref[0] = down_ref[...].astype(F32)
    shard_ref[1] = up_ref[...].astype(F32)
    table[pl.ds(0, PAD), :] = jnp.zeros((PAD, E), F32)
    cold[pl.ds(0, PAD), :] = jnp.zeros((PAD, E), F32)
    inc[:, PAIRS:] = jnp.zeros((N_DP, SLOTS // 2 - PAIRS, 2, E), BF16)

    sub = iota((B, B), 0)
    lane = iota((B, B), 1)
    lane_row = iota((1, B), 1)
    before = jnp.where(sub < lane, 1.0, 0.0).astype(BF16)
    count = jnp.zeros((N_DP, 1), F32)
    codes = jnp.zeros((4 * N_DP, B), F32)
    for j in range(NC):
        spot_n = ((owner_ref[j : j + 1, :] - me + N_DP) * UNSHIFT) & (N_DP - 1)
        hit = jnp.where(sub == spot_n, 1.0, 0.0)
        rank = jnp.dot(hit.astype(BF16), before, preferred_element_type=F32) + count
        slot = jnp.sum(hit * rank, axis=0, keepdims=True).astype(I32)
        count = count + jnp.sum(hit, axis=1, keepdims=True)
        place[j : j + 1, :] = spot_n * SLOTS + jnp.clip(slot, 0, CAP - 1)
        at = jnp.where(sub == slot + SLOTS * (spot_n & 3), 1.0, 0.0).astype(BF16)
        row = rows_ref[j : j + 1, :] + PAD
        number = lane_row + (j * B + PAD)
        parts = [(hit * v.astype(F32)).astype(BF16) for v in (row >> 5, row & 31, number >> 5, number & 31)]
        codes = codes + lax.dot_general(jnp.concatenate(parts, axis=0), at, NT, preferred_element_type=F32)
    req[:, 0, :] = jnp.clip((codes[:N_DP] * 32.0 + codes[N_DP : 2 * N_DP]).astype(I32), 0, OWN + PAD - 1)
    inverse[...] = jnp.clip((codes[2 * N_DP : 3 * N_DP] * 32.0 + codes[3 * N_DP :]).astype(I32), 0, NC * B + PAD - 1)
    pl.semaphore_wait(barrier, N_DP + N_X - 2)

    def line_send(k, carry):
        to = lax.rem(spot + k, LINE)
        remote(shard_ref.at[lax.rem(to, 2)], line.at[spot], line_s, line_r, (y * LINE + to, x)).start()
        return carry

    lax.fori_loop(1, LINE, line_send, 0)
    line[pl.ds(spot, 1)] = shard_ref[pl.ds(core, 1)]

    def ask(n, carry):
        to = lax.rem(me + n * SHIFT, N_DP)
        remote(req.at[n], asked.at[n], req_s, req_r, (to, x)).start()
        return carry

    lax.fori_loop(1, N_DP, ask, 0)
    asked[0] = req[0]
    place_copy = pltpu.make_async_copy(place, place_s, load.at[4])
    place_copy.start()
    inverse_copy = pltpu.make_async_copy(inverse, inverse_s, load.at[5])
    inverse_copy.start()

    some = pl.ds(0, LINE - 1)
    remote(line.at[some], line.at[some], line_s, line_r, sibling).wait()
    weights[core, x * N_Y + y] = line[...].reshape(LINE, F).astype(BF16)

    def block(bx, by):
        return weights.at[core, lax.rem(bx + N_X, N_X) * N_Y + lax.rem(by + N_Y, N_Y)]

    def y_up(s):
        return remote(block(x, y - s), block(x, y - s), up_s.at[s], up_r.at[s], (lax.rem(y + 1, N_Y) * LINE + spot, x))

    def y_dn(s):
        return remote(block(x, y + s), block(x, y + s), dn_s.at[s], dn_r.at[s], (lax.rem(y + N_Y - 1, N_Y) * LINE + spot, x))

    shifts = (0, -1, 1, -2, 2, -3, 3, -4)

    def xp(k):
        return remote(block(x, y + shifts[k]), block(x, y + shifts[k]), xp_s.at[k], xp_r.at[k], (me, lax.rem(x + 1, N_X)))

    def xm(k):
        return remote(block(x, y + shifts[k]), block(x, y + shifts[k]), xm_s.at[k], xm_r.at[k], (me, lax.rem(x + N_X - 1, N_X)))

    def x2(k):
        if k % 2 == 0:
            ref, to = block(x - 1, y + shifts[k]), lax.rem(x + 1, N_X)
        else:
            ref, to = block(x + 1, y + shifts[k]), lax.rem(x + N_X - 1, N_X)
        return remote(ref, ref, x2_s.at[k], x2_r.at[k], (me, to))

    def sib(dx, k):
        ref = block(x + dx, y + shifts[k])
        n = (dx % N_X) * N_Y + k
        return remote(ref, ref, sib_s.at[n], sib_r.at[n], sibling)

    def have(k):
        xp(k).start()
        xm(k).start()
        sib(0, k).start()

    y_up(0).start()
    y_dn(0).start()
    have(0)

    most = pl.ds(0, N_DP - 1)
    remote(req.at[most], asked.at[most], req_s, req_r, sibling).wait()
    ask_copy = pltpu.make_async_copy(asked, ask_s, load.at[6])
    ask_copy.start()
    loads[0].wait()
    ask_copy.wait()
    sent = pl.ds(0, PAIRS)

    def gather(n, source, index):
        last = source.shape[0] - 1
        picked = [source[pl.ds(jnp.clip(index(i), 0, last), 1), :] for i in range(CAP)]
        full = jnp.concatenate(picked + [jnp.zeros((SLOTS - CAP, E), F32)], axis=0)
        snd[pl.ds(n, 1)] = full.astype(BF16).reshape(1, SLOTS // 2, 2, E)

    def answer(n, carry):
        corner = lax.rem(n, 4) * SLOTS
        gather(n, table, lambda i: ask_s[n, 0, corner + i])
        to = lax.rem(me + n * (N_DP - SHIFT), N_DP)
        remote(snd.at[n, sent], ret.at[n, sent], row_s, row_r, (to, x)).start()
        return carry

    for s in range(1, 5):
        lax.fori_loop(max(1, (s - 1) * 32), s * 32, answer, 0)
        y_up(s - 1).wait_recv()
        if s < 4:
            y_up(s).start()
        have(2 * s - 1)
        if s < 4:
            y_dn(s - 1).wait_recv()
            if s < 3:
                y_dn(s).start()
            have(2 * s)

    loads[1].wait()
    low_table = hot_table[...].astype(BF16)
    number = iota((B, HOT), 1).astype(F32)
    height = iota((HOT, B), 0)

    def hot_slot(j):
        ids = hot_rows[j : j + 1, :]
        column = jnp.transpose(jnp.broadcast_to(ids.astype(F32), (B, B)))
        wide = jnp.concatenate([column] * (HOT // B), axis=1)
        one = jnp.where(wide == number, 1.0, 0.0).astype(BF16)
        x0[:, j * E : (j + 1) * E] = jnp.dot(one, low_table, preferred_element_type=F32).astype(BF16)
        pick[:, j * B : (j + 1) * B] = jnp.where(height == ids, 1.0, 0.0).astype(BF16)

    for k in range(N_Y):
        xp(k).wait_recv()
        if k % 2 == 0:
            x2(k).start()
        sib(-1, k).start()
        xm(k).wait_recv()
        if k % 2 == 1:
            x2(k).start()
        sib(1, k).start()
        hot_slot(k)
    for j in range(N_Y, NH):
        hot_slot(j)

    gather(0, table, lambda i: ask_s[0, 0, i])
    ret[0, sent] = snd[0, sent]
    remote(snd.at[most, sent], ret.at[most, sent], row_s, row_r, sibling).wait()
    rows[...] = ret[...].reshape(N_DP * SLOTS, E).astype(F32)
    place_copy.wait()
    inverse_copy.wait()
    for j in range(NC):

        def fetch(b, carry, j=j):
            at = jnp.clip(place_s[j, b], 0, N_DP * SLOTS - 1)
            cold[pl.ds(PAD + j * B + b, 1), :] = rows[pl.ds(at, 1), :]
            return carry

        lax.fori_loop(0, B, fetch, 0, unroll=16)
    for j in range(NC):
        x0[:, (NH + j) * E : (NH + j + 1) * E] = cold[PAD + j * B : PAD + (j + 1) * B, :].astype(BF16)

    for k in range(N_Y):
        x2(k).wait_recv()
        sib(2, k).start()
    for s in range(4):
        y_up(s).wait_send()
    for s in range(3):
        y_dn(s).wait_send()
    for k in range(N_Y):
        xp(k).wait_send()
        xm(k).wait_send()
        x2(k).wait_send()
    for dx in range(N_X):
        for k in range(N_Y):
            sib(dx, k).wait()

    bias = affine[0:1, :]
    gain = affine[1:2, :]
    down = weights.at[0]
    above = weights.at[1]
    hid = lax.dot_general(x0[...], down[...].reshape(R, F), NT, preferred_element_type=F32).astype(BF16)
    logit = jnp.zeros((B, 1), F32)
    wide = 256
    for n in range(F // wide):
        cut = slice(n * wide, (n + 1) * wide)
        u = jnp.dot(hid, above[:, :, cut].reshape(R, wide), preferred_element_type=F32) + bias[:, cut]
        upper[:, cut] = u
        xf = x0[:, cut].astype(F32)
        logit = logit + jnp.sum((xf * u + xf) * gain[:, cut], axis=1, keepdims=True)
    label = jnp.transpose(jnp.broadcast_to(labels[...].astype(F32), (B, B)))[:, 0:1]
    delta = jax.nn.sigmoid(logit) - label
    d_hid = jnp.zeros((B, R), F32)
    for n in range(F // wide):
        cut = slice(n * wide, (n + 1) * wide)
        d_up = ((delta * gain[:, cut]) * x0[:, cut].astype(F32)).astype(BF16)
        d_hid = d_hid + lax.dot_general(d_up, above[:, :, cut].reshape(R, wide), NT, preferred_element_type=F32)
    d_hid = d_hid.astype(BF16)

    def slots(n):
        cut = slice(n * wide, (n + 1) * wide)
        grad = (delta * gain[:, cut]) * (upper[:, cut] + 1.0) + jnp.dot(
            d_hid, down[:, :, cut].reshape(R, wide), preferred_element_type=F32
        )
        for half in range(2):
            j = 2 * n + half
            value = grad[:, half * E : (half + 1) * E]
            if j < NH:
                first = value.astype(BF16)
                split[j * B : (j + 1) * B, :E] = first
                split[j * B : (j + 1) * B, E:] = (value - first.astype(F32)).astype(BF16)
            else:
                cold[PAD + (j - NH) * B : PAD + (j - NH + 1) * B, :] = value

    for n in reversed(range(NH // 2, F // wide)):
        slots(n)

    def give(n, carry):
        corner = lax.rem(n, 4) * SLOTS
        gather(n, cold, lambda i: inverse_s[n, corner + i])
        to = lax.rem(me + n * SHIFT, N_DP)
        batch = n // 32
        remote(snd.at[n, sent], inc.at[n, sent], inc_s.at[batch], inc_r.at[batch], (to, x)).start()
        return carry

    lax.fori_loop(1, N_DP, give, 0)
    gather(0, cold, lambda i: inverse_s[0, i])
    inc[0, sent] = snd[0, sent]

    for n in range(NH // 2):
        slots(n)
    both = jnp.dot(pick[...], split[...], preferred_element_type=F32)
    hot_part[...] = both[:, :E] + both[:, E:]
    half, quarter, thin = HOT // 2, HOT // 8, HOT // 64
    swap = remote(hot_part.at[pl.ds((1 - core) * half, half)], from_core, hs.at[0], hr.at[0], sibling)
    swap.start()

    one, zero = jnp.ones((), BF16), jnp.zeros((), BF16)
    chunk = OWN // N_X

    def batch_ids(b):
        ids = [jnp.sum(asked[pl.ds(b * 32 + 4 * q, 4)], axis=0) - PAD for q in range(8)]
        return jnp.concatenate(ids, axis=1).astype(F32)

    def batch_sum(ids, b, first):
        tall = iota((256, B), 0).astype(F32).astype(BF16)
        halves = []
        for r in range(chunk // 256):
            near = (ids - (first + 256 * r).astype(F32)).astype(BF16)
            halves.append(
                jnp.concatenate(
                    [jnp.where(tall == near[:, q * B : (q + 1) * B], one, zero) for q in range(8)], axis=1
                )
            )
        values = inc[b * 32 : (b + 1) * 32].reshape(32 * SLOTS, E)
        return jnp.dot(jnp.concatenate(halves, axis=0), values, preferred_element_type=F32)

    def batch_wait(b):
        got = pl.ds(32 * b, 32) if b else pl.ds(1, 31)
        remote(snd.at[got, sent], inc.at[got, sent], inc_s.at[b], inc_r.at[b], sibling).wait()

    def batch(b):
        batch_wait(b)
        ids = batch_ids(b)

        def add(c, carry):
            here = pl.ds(pl.multiple_of(c * chunk, chunk), chunk)
            value = batch_sum(ids, b, c * chunk)
            acc[here, :] = value if b == 0 else acc[here, :] + value
            return carry

        lax.fori_loop(0, N_X, add, 0)

    swap.wait()
    mine[...] = hot_part[pl.ds(pl.multiple_of(core * half, half), half), :] + from_core[...]
    for d in range(1, N_X):
        to = lax.rem(x + d, N_X)
        remote(mine.at[pl.ds(to * quarter, quarter)], from_x.at[x], hs.at[1], hr.at[1], (me, to)).start()
    from_x[pl.ds(x, 1)] = mine[pl.ds(x * quarter, quarter), :].reshape(1, quarter, E)
    batch(0)
    remote(from_x.at[pl.ds(0, N_X - 1)], from_x.at[pl.ds(0, N_X - 1)], hs.at[1], hr.at[1], sibling).wait()
    line_sum[...] = (from_x[0] + from_x[1]) + (from_x[2] + from_x[3])
    for d in range(1, N_Z):
        to = lax.rem(z + d, N_Z)
        remote(
            line_sum.at[pl.ds(to * thin, thin)], from_z.at[z], hs.at[2], hr.at[2], (y * LINE + to * 2 + core, x)
        ).start()
    from_z[pl.ds(z, 1)] = line_sum[pl.ds(z * thin, thin), :].reshape(1, thin, E)
    batch(1)
    remote(from_z.at[pl.ds(0, N_Z - 1)], from_z.at[pl.ds(0, N_Z - 1)], hs.at[2], hr.at[2], sibling).wait()
    tiny[...] = jnp.sum(from_z[...], axis=0)
    for d in range(1, N_Y):
        to = lax.rem(y + d, N_Y)
        remote(tiny, from_y.at[y], hs.at[3], hr.at[3], (to * LINE + spot, x)).start()
    from_y[pl.ds(y, 1)] = tiny[...].reshape(1, thin, E)
    batch(2)
    remote(from_y.at[pl.ds(0, N_Y - 1)], from_y.at[pl.ds(0, N_Y - 1)], hs.at[3], hr.at[3], sibling).wait()
    total = jnp.sum(from_y[...], axis=0)
    base = core * half + x * quarter + z * thin
    spot_rows = pl.ds(pl.multiple_of(base, thin), thin)
    loads[2].wait()
    loads[3].wait()
    new_hot[spot_rows, :] = compensate(hot_table[spot_rows, :], hot_backup[spot_rows, :], total, rate_hot)
    for d in range(1, N_Z):
        to = lax.rem(z + d, N_Z)
        remote(
            new_hot.at[spot_rows], new_hot.at[spot_rows], hs.at[4], hr.at[4], (y * LINE + to * 2 + core, x)
        ).start()

    def send_part(d):
        return remote(part.at[d - 1], from_part.at[d - 1], ps.at[d - 1], pr.at[d - 1], (me, lax.rem(x + d, N_X)))

    batch_wait(3)
    ids = batch_ids(3)

    def finish(d):
        which = lax.rem(x + d, N_X) * chunk
        return acc[pl.ds(pl.multiple_of(which, chunk), chunk), :] + batch_sum(ids, 3, which)

    for d in (2, 1, 3):
        part[d - 1] = finish(d).astype(BF16)
        send_part(d).start()
    total_cold = finish(0)
    remote(
        new_hot.at[pl.ds(0, (N_Z - 1) * thin)], new_hot.at[pl.ds(0, (N_Z - 1) * thin)], hs.at[4], hr.at[4], sibling
    ).wait()
    x_rows = pl.ds(pl.multiple_of(core * half + x * quarter, quarter), quarter)
    for d in range(1, N_X):
        to = lax.rem(x + d, N_X)
        remote(new_hot.at[x_rows], new_hot.at[x_rows], gs.at[0], gr.at[0], (me, to)).start()
    for d in (2, 1, 3):
        send_part(d).wait()
        total_cold = total_cold + from_part[d - 1].astype(F32)

    def cold_rows(dx, start, size):
        first = lax.rem(x + dx + N_X, N_X) * chunk + start
        return pl.ds(pl.multiple_of(first, size), size)

    own = cold_rows(0, 0, chunk)
    own_table = table[pl.ds(pl.multiple_of(x * chunk + PAD, PAD), chunk), :]
    new_cold[own, :] = compensate(own_table, cold_backup[own, :], total_cold, rate_cold)

    def pass_on(n, span, step):
        return remote(new_cold.at[span], new_cold.at[span], as_.at[n], ar.at[n], (me, lax.rem(x + step, N_X)))

    right = pass_on(0, own, 1)
    left = pass_on(1, own, N_X - 1)
    right.start()
    left.start()
    remote(
        new_hot.at[pl.ds(0, (N_X - 1) * quarter)], new_hot.at[pl.ds(0, (N_X - 1) * quarter)], gs.at[0], gr.at[0], sibling
    ).wait()
    core_rows = pl.ds(pl.multiple_of(core * half, half), half)
    last = remote(new_hot.at[core_rows], new_hot.at[core_rows], gs.at[1], gr.at[1], sibling)
    last.start()
    right.wait_recv()
    right2 = pass_on(2, cold_rows(-1, 0, chunk // 2), 1)
    right2.start()
    left.wait_recv()
    left2 = pass_on(3, cold_rows(1, chunk // 2, chunk // 2), N_X - 1)
    left2.start()
    right.wait_send()
    left.wait_send()
    right2.wait()
    left2.wait()
    last.wait()


VMEM = pl.BlockSpec(memory_space=pltpu.VMEM)
HBM = pl.BlockSpec(memory_space=pltpu.HBM)
DMA = pltpu.SemaphoreType.DMA


def shards(
    hot_ids, cold_rows, cold_owner, labels, hot_table, hot_backup,
    cold_table, cold_backup, cross_down, cross_up, cross_bias, out_weight,
):
    rows = hot_ids.shape[0]
    n_data = lax.axis_size("dp")
    n_reps = lax.axis_size("rep")
    batch_all = rows * n_data * n_reps
    rate_hot = 20.0 * math.sqrt(HOT / (batch_all * NH))
    rate_cold = 20.0 * math.sqrt(OWN * n_data / (batch_all * NC))

    owner = cold_owner.reshape(B, NC).T
    affine = jnp.stack([cross_bias, out_weight])

    def kernel(*refs):
        step_kernel(rate_hot, rate_cold, *refs)

    return pl.pallas_call(
        kernel,
        out_shape=(
            jax.ShapeDtypeStruct((HOT, E), F32),
            jax.ShapeDtypeStruct((OWN, E), F32),
        ),
        in_specs=[VMEM] * 7 + [HBM] * 4,
        out_specs=(VMEM, VMEM),
        scratch_shapes=[
            pltpu.VMEM((OWN, E), BF16),
            pltpu.VMEM((HOT, E), F32),
            pltpu.VMEM((HOT, E), BF16),
            pltpu.VMEM((OWN + PAD, E), F32),
            pltpu.VMEM((N_DP, 1, B), I32),
            pltpu.VMEM((N_DP, 1, B), I32),
            pltpu.VMEM((NC, B), I32),
            pltpu.VMEM((N_DP, B), I32),
            pltpu.SMEM((N_DP, 1, B), I32),
            pltpu.SMEM((NC, B), I32),
            pltpu.SMEM((N_DP, B), I32),
            pltpu.VMEM((N_DP, SLOTS // 2, 2, E), BF16),
            pltpu.VMEM((N_DP, SLOTS // 2, 2, E), BF16),
            pltpu.VMEM((N_DP, SLOTS // 2, 2, E), BF16),
            pltpu.VMEM((LINE, 1, F), F32),
            pltpu.VMEM((2, 1, F), F32),
            pltpu.VMEM((2, N_X * N_Y, LINE, F), BF16),
            pltpu.VMEM((N_DP * SLOTS, E), F32),
            pltpu.VMEM((B, F), BF16),
            pltpu.VMEM((NC * B + PAD, E), F32),
            pltpu.VMEM((B, F), F32),
            pltpu.VMEM((HOT, NH * B), BF16),
            pltpu.VMEM((NH * B, 2 * E), BF16),
            pltpu.VMEM((HOT, E), F32),
            pltpu.VMEM((OWN, E), F32),
            pltpu.VMEM((HOT // 2, E), F32),
            pltpu.VMEM((HOT // 2, E), F32),
            pltpu.VMEM((N_X, HOT // 8, E), F32),
            pltpu.VMEM((HOT // 8, E), F32),
            pltpu.VMEM((N_Z, HOT // 64, E), F32),
            pltpu.VMEM((HOT // 64, E), F32),
            pltpu.VMEM((N_Y, HOT // 64, E), F32),
            pltpu.VMEM((3, OWN // N_X, E), BF16),
            pltpu.VMEM((3, OWN // N_X, E), BF16),
            DMA((7,)), DMA, DMA, DMA, DMA, DMA, DMA,
            DMA((4,)), DMA((4,)), DMA((3,)), DMA((3,)),
            DMA((8,)), DMA((8,)), DMA((8,)), DMA((8,)), DMA((8,)), DMA((8,)), DMA((32,)), DMA((32,)),
            DMA((4,)), DMA((4,)), DMA((5,)), DMA((5,)), DMA((2,)), DMA((2,)),
            DMA((3,)), DMA((3,)), DMA((4,)), DMA((4,)),
        ],
        compiler_params=pltpu.CompilerParams(
            collective_id=0, has_side_effects=True, vmem_limit_bytes=60 << 20
        ),
        name="step",
    )(
        owner, cold_rows.T, cross_down.reshape(1, F), cross_up, hot_ids.T, labels.reshape(1, B), affine,
        cold_table, cold_backup, hot_table, hot_backup,
    )


def solution(mesh):
    placed = (
        P(("dp", "rep"), None),
        P(("dp", "rep"), None),
        P(("dp", "rep"), None),
        P(("dp", "rep")),
        P(),
        P(),
        P("dp", None),
        P("dp", None),
        P(None, ("dp", "rep")),
        P(("dp", "rep"), None),
        P(),
        P(),
    )
    return jax.shard_map(
        shards, mesh=mesh, in_specs=placed, out_specs=(P(), P("dp", None)), check_vma=False
    )
```
